256 devices in a mesh: tx: 32 (over z, y), ty: 8 (over x, core).
Axes of the slice: x: 4, y: 4, z: 8, core: 2. Of those that a mesh axis runs over, the one named last changes fastest.
Arguments:
- probes: bfloat16 [4096, 1024, 128], P('tx', 'ty')
- filter_taps: float32 [2, 2, 33], replicated, may hold values from 0.05 to 1
- cluster_ranks: int32 [5, 32, 8], replicated, may hold values from 64 to 128
Outputs:
- leaf_basis: bfloat16 [4096, 1024, 128], P('tx', 'ty')
- transfers: float32 [32, 8, 4, 128, 128], P('tx', 'ty')
The draws below stay inside these ranges and needn't reach their ends.
Inputs may be any that keep to these rules, and one draw needn't show every extreme that they name: `cluster_ranks`: only the entry of a cluster's first leaf (lowest row and column indices) is its rank at that level.
All inputs are finite; a program needn't handle non-finite values.
Results may differ from the reference program's by a relative error of at most 0.014.
The reference program's roundings to bfloat16 on the way (of `combined`, `middle`, `sketch` and `weights`) count: a program that leaves them out, or rounds other values in their place, can miss the bound.
Values may be sent and summed in bfloat16 or wider, within the bound.
A program may use at most 128 MiB of HBM per device.

```python
import math
import jax
import jax.numpy as jnp
from jax import lax

TILE = 128
P_SIZE = 128
TAPS = 33
LEVELS = 4
REACH = 80
NX = 4096
NY = 1024
N_TX = 32
N_TY = 8


def draw_probes(key, part):
    first_key, second_key, third_key = jax.random.split(key, 3)
    blocks_x = NX // TILE
    blocks_y = NY // TILE
    half = P_SIZE // 2
    spread = jax.random.uniform(first_key, (blocks_x, blocks_y), jnp.float32, 0.0, math.log(10.0))
    noise = jnp.clip(jax.random.normal(second_key, (NX, NY, P_SIZE), jnp.float32), -6.0, 6.0)
    shared = jnp.clip(jax.random.normal(third_key, (NX, NY), jnp.float32), -6.0, 6.0)
    channel = jnp.arange(P_SIZE).astype(jnp.float32)
    steps_down = -2.0 * channel / max(half - 1, 1)
    own_scale = jnp.where(channel < half, jnp.power(10.0, steps_down), 1.0)
    shared_scale = jnp.where(channel < half, 1.0 / math.sqrt(half), 0.0)
    values = noise * own_scale[None, None, :] + shared[:, :, None] * shared_scale[None, None, :]
    scales = jnp.exp(spread)
    scales = jnp.repeat(jnp.repeat(scales, TILE, axis=0), TILE, axis=1)
    return (values * scales[:, :, None]).astype(jnp.bfloat16)


def place_ends(entries, own_key, smallest, high):
    dims = entries.shape
    place = [jax.random.randint(jax.random.fold_in(own_key, axis), (), 0, dims[axis]) for axis in range(len(dims))]
    entries = entries.at[tuple(place)].set(smallest)
    longest = dims.index(max(dims))
    place[longest] = (place[longest] + 1) % dims[longest]
    return entries.at[tuple(place)].set(high)


def setup_inputs(seed: int = 0) -> dict:
    streams_of = jax.random.split(jax.random.key(seed), 4)
    return {
        "probes": draw_probes(jax.random.fold_in(streams_of[3], 71), 0),
        "filter_taps": jnp.clip(jnp.exp(jax.random.uniform(streams_of[1], (2, 2, TAPS), jnp.float32, math.log(0.05), math.log(1.0))), 0.05, 1.0),
        "cluster_ranks": place_ends(jax.random.randint(streams_of[2], (LEVELS + 1, N_TX, N_TY), P_SIZE // 2, P_SIZE + 1), jax.random.fold_in(streams_of[2], 1), P_SIZE // 2, P_SIZE).astype(jnp.int32),
    }


def solve_triangular(matrix, right, lower):
    return jax.scipy.linalg.solve_triangular(matrix, right, lower=lower)

def composite(filter_taps):
    count = filter_taps.shape[-1]
    wide = 5 * (count - 1) + 1
    first = jnp.arange(count)[:, None, None]
    second = jnp.arange(count)[None, :, None]
    spot = jnp.arange(wide)[None, None, :]
    table = (first + 4 * second == spot).astype(jnp.float32)
    outer = filter_taps[:, 0, :, None] * filter_taps[:, 1, None, :]
    return jnp.einsum('dab,abm->dm', outer, table, precision=lax.Precision.HIGHEST).astype(jnp.bfloat16)

def factor(gram, keep_mask):
    outer = keep_mask[..., :, None] * keep_mask[..., None, :]
    masked = gram * outer
    trace_sum = jnp.sum(jnp.diagonal(masked, axis1=-2, axis2=-1), axis=-1)
    delta = 0.01 * trace_sum / jnp.sum(keep_mask, axis=-1)
    ident = jnp.eye(gram.shape[-1], dtype=jnp.float32)
    shifted = masked + ident * (1.0 - keep_mask)[..., None, :] + delta[..., None, None] * ident * keep_mask[..., None, :]
    return (masked, jnp.linalg.cholesky(shifted))

def products(zeta):
    return jnp.einsum('...kp,...kq->...pq', zeta, zeta, precision=lax.Precision.HIGHEST)

def transfer(lower, keep_mask, child_z):
    right = keep_mask[..., :, None] * jnp.swapaxes(child_z, -1, -2)
    return jnp.swapaxes(solve_triangular(lower, right, lower=True), -1, -2)

def rank_mask(rank_value, width):
    return (jnp.arange(width) < rank_value[..., None]).astype(jnp.float32)

def convolve(probes, combined):
    kernel_x = combined[0].astype(jnp.float32).reshape(1, 1, -1, 1)
    kernel_y = combined[1].astype(jnp.float32).reshape(1, 1, 1, -1)
    groups = probes.reshape(NX, NY, P_SIZE // 8, 8)

    def one_group(index):
        block = lax.dynamic_index_in_dim(groups, index, 2, keepdims=False)
        field = jnp.transpose(block, (2, 0, 1))[:, None].astype(jnp.float32)
        middle = lax.conv_general_dilated(field, kernel_x, (1, 1), ((REACH, REACH), (0, 0)), precision=lax.Precision.HIGHEST)
        middle = lax.optimization_barrier(middle.astype(jnp.bfloat16)).astype(jnp.float32)
        result = lax.conv_general_dilated(middle, kernel_y, (1, 1), ((0, 0), (REACH, REACH)), precision=lax.Precision.HIGHEST)
        return result[:, 0].astype(jnp.bfloat16)
    stacked = lax.map(one_group, jnp.arange(P_SIZE // 8, dtype=jnp.int32))
    return jnp.transpose(stacked.reshape(P_SIZE, NX, NY), (1, 2, 0))

def reference(probes, filter_taps, cluster_ranks):
    combined = composite(filter_taps)
    sketch = convolve(probes, combined)
    tiles = sketch.reshape(N_TX, TILE, N_TY, TILE, P_SIZE)

    def tile_gram(block):
        wide_block = block.astype(jnp.float32)
        return jnp.einsum('ibjp,ibjq->bpq', wide_block, wide_block, precision=lax.Precision.HIGHEST)
    gram = lax.map(tile_gram, tiles) / (TILE * TILE)
    keep_mask = rank_mask(cluster_ranks[0], P_SIZE)
    masked, lower = factor(gram, keep_mask)
    diag_mask = jnp.eye(P_SIZE, dtype=jnp.float32) * keep_mask[..., None, :]
    weights = jnp.swapaxes(solve_triangular(lower, diag_mask, lower=True), -1, -2).astype(jnp.bfloat16)

    def tile_basis(pair):
        block, weight = pair
        return jnp.einsum('ibjp,bpq->ibjq', block.astype(jnp.float32), weight.astype(jnp.float32), precision=lax.Precision.HIGHEST).astype(jnp.bfloat16)
    leaf_basis = lax.map(tile_basis, (tiles, weights)).reshape(NX, NY, P_SIZE)
    zeta = solve_triangular(lower, masked, lower=True)
    grams = products(zeta)
    span_x, span_y = (1, 1)
    results = []
    for level in range(1, 5):
        if level % 2 == 1:
            merged = (grams[0::2] + grams[1::2]) * 0.5
            next_x, next_y, along = (span_x * 2, span_y, 0)
        else:
            merged = (grams[:, 0::2] + grams[:, 1::2]) * 0.5
            next_x, next_y, along = (span_x, span_y * 2, 1)
        keep_mask = rank_mask(cluster_ranks[level, ::next_x, ::next_y], P_SIZE)
        masked, lower = factor(merged, keep_mask)
        lower_child = jnp.repeat(lower, 2, axis=along)
        mask_child = jnp.repeat(keep_mask, 2, axis=along)
        moved = transfer(lower_child, mask_child, zeta)
        results.append(jnp.repeat(jnp.repeat(moved, span_x, axis=0), span_y, axis=1))
        zeta = solve_triangular(lower, masked, lower=True)
        grams = products(zeta)
        span_x, span_y = (next_x, next_y)
    return (leaf_basis, jnp.stack(results, axis=2))
```

```python
import functools

import jax
import jax.numpy as jnp
from jax import lax
from jax.experimental import pallas as pl
from jax.experimental.pallas import tpu as pltpu
from jax.sharding import PartitionSpec as P

HIGHEST = lax.Precision.HIGHEST
PANEL = 16


def extended(block, sides, width):
    for axis, dim in sides:
        count = lax.axis_size(axis)
        forward = [(i, i + 1) for i in range(count - 1)]
        backward = [(target, source) for source, target in forward]
        low = lax.ppermute(
            lax.slice_in_dim(block, block.shape[dim] - width, None, axis=dim), axis, forward
        )
        high = lax.ppermute(lax.slice_in_dim(block, 0, width, axis=dim), axis, backward)
        block = jnp.concatenate([low, block, high], axis=dim)
    return block


def from_partner(shard, axis, stride):
    return lax.ppermute(shard, axis, [(i, i ^ 1 << stride) for i in range(lax.axis_size(axis))])


def composite(filter_taps):
    count = filter_taps.shape[-1]
    wide = 5 * (count - 1) + 1
    first = jnp.arange(count)[:, None, None]
    second = jnp.arange(count)[None, :, None]
    spot = jnp.arange(wide)[None, None, :]
    table = (first + 4 * second == spot).astype(jnp.float32)
    outer = filter_taps[:, 0, :, None] * filter_taps[:, 1, None, :]
    return jnp.einsum("dab,abm->dm", outer, table, precision=HIGHEST).astype(jnp.bfloat16)


def toeplitz(line_taps, length):
    wide = line_taps.shape[0]
    columns = length + wide - 1
    pattern = jnp.concatenate([line_taps, jnp.zeros((length,), line_taps.dtype)])
    return jnp.tile(pattern, length)[: length * columns].reshape(length, columns)


def eliminate(work, size):
    at_row = lax.broadcasted_iota(jnp.int32, (PANEL, size), 0)
    for start in range(0, size, PANEL):
        left = work[pl.ds(start, PANEL), pl.ds(0, size)]
        right = work[pl.ds(start, PANEL), pl.ds(size, size)]
        columns = [
            jnp.broadcast_to(left[:, start + j : start + j + 1], (PANEL, size))
            for j in range(PANEL)
        ]
        scale = jnp.zeros((PANEL, size), jnp.float32)
        for j in range(PANEL):
            pivot = columns[j][j : j + 1, :]
            below = jnp.where(at_row > j, columns[j] * (1.0 / pivot), 0.0)
            for k in range(j + 1, PANEL):
                columns[k] = columns[k] - below * columns[k][j : j + 1, :]
            left = left - below * left[j : j + 1, :]
            right = right - below * right[j : j + 1, :]
            scale = jnp.where(at_row == j, lax.rsqrt(pivot), scale)
        left = left * scale
        right = right * scale
        work[pl.ds(start, PANEL), pl.ds(size, size)] = right
        rest = size - start - PANEL
        if rest:
            tall = left.T[start + PANEL :, :]
            both = jnp.concatenate([left, right], axis=1)
            below = pl.ds(start + PANEL, rest)
            work[below, :] = work[below, :] - jnp.dot(
                tall, both, precision=HIGHEST, preferred_element_type=jnp.float32
            )


def factor_kernel(grams, scale, rank_ref, *refs):
    gram_refs = refs[:grams]
    inverse_ref, zeta_ref, product_ref, work = refs[grams:]
    size = inverse_ref.shape[0]
    rank = rank_ref[0]
    row = lax.broadcasted_iota(jnp.int32, (size, size), 0)
    col = lax.broadcasted_iota(jnp.int32, (size, size), 1)
    gram = gram_refs[0][...]
    for other in gram_refs[1:]:
        gram = gram + other[...]
    masked = jnp.where((row < rank) & (col < rank), gram * scale, 0.0)
    on_diagonal = row == col
    trace = jnp.sum(
        jnp.sum(jnp.where(on_diagonal, masked, 0.0), axis=0, keepdims=True), axis=1, keepdims=True
    )
    delta = 0.01 * trace / rank.astype(jnp.float32)
    shift = jnp.where(row < rank, jnp.broadcast_to(delta, (size, size)), 1.0)
    work[:, pl.ds(0, size)] = masked + jnp.where(on_diagonal, shift, 0.0)
    work[:, pl.ds(size, size)] = jnp.where(on_diagonal, 1.0, 0.0)
    eliminate(work, size)
    inverse = work[:, pl.ds(size, size)]
    zeta = jnp.dot(inverse, masked, precision=HIGHEST, preferred_element_type=jnp.float32)
    zeta_ref[...] = zeta
    product_ref[...] = lax.dot_general(
        zeta,
        zeta,
        (((0,), (0,)), ((), ())),
        precision=HIGHEST,
        preferred_element_type=jnp.float32,
    )
    inverse_ref[...] = jnp.where(col < rank, inverse, 0.0)


def factor(grams, scale, rank):
    size = grams[0].shape[0]
    square = jax.ShapeDtypeStruct((size, size), jnp.float32)
    whole = pl.BlockSpec(memory_space=pltpu.VMEM)
    return pl.pallas_call(
        functools.partial(factor_kernel, len(grams), scale),
        out_shape=(square,) * 3,
        in_specs=[pl.BlockSpec(memory_space=pltpu.SMEM)] + [whole] * len(grams),
        out_specs=(whole,) * 3,
        scratch_shapes=[pltpu.VMEM((size, 2 * size), jnp.float32)],
        compiler_params=pltpu.CompilerParams(vmem_limit_bytes=8 << 20),
        name="factor",
    )(rank.reshape(1), *grams)


def transfer(inverse, child_z):
    return jnp.einsum("qk,pk->qp", child_z, inverse, precision=HIGHEST)


def local(probes, filter_taps, cluster_ranks):
    combined = composite(filter_taps)
    reach = (combined.shape[1] - 1) // 2
    rows, cols, width = probes.shape
    row_at = lax.axis_index("tx")
    col_at = lax.axis_index("ty")
    tall = extended(probes, (("tx", 0),), reach)
    middle = jnp.dot(
        toeplitz(combined[0], rows),
        tall.reshape(tall.shape[0], cols * width),
        preferred_element_type=jnp.float32,
    )
    middle = middle.reshape(rows, cols, width).astype(jnp.bfloat16)
    broad = extended(middle, (("ty", 1),), reach)
    sketch = jnp.einsum(
        "yc,xcp->xyp", toeplitz(combined[1], cols), broad, preferred_element_type=jnp.float32
    ).astype(jnp.bfloat16)
    flat = sketch.reshape(rows * cols, width)
    gram = jnp.einsum("np,nq->pq", flat, flat, preferred_element_type=jnp.float32)
    inverse, zeta, product = factor((gram,), 1.0 / (rows * cols), cluster_ranks[0, row_at, col_at])
    moved = []
    span = {"tx": 1, "ty": 1}
    for level in range(1, cluster_ranks.shape[0]):
        axis = "tx" if level % 2 else "ty"
        partner = from_partner(product, axis, span[axis].bit_length() - 1)
        span[axis] *= 2
        rank = cluster_ranks[
            level, row_at - row_at % span["tx"], col_at - col_at % span["ty"]
        ]
        if level == 1:
            leaf_basis = (
                jnp.dot(flat, inverse.T.astype(jnp.bfloat16), preferred_element_type=jnp.float32)
                .astype(jnp.bfloat16)
                .reshape(rows, cols, width)
            )
        child_z = zeta
        inverse, zeta, product = factor((product, partner), 0.5, rank)
        moved.append(transfer(inverse, child_z))
    return (leaf_basis, jnp.stack(moved, axis=0)[None, None])


def solution(mesh):
    in_specs = (P("tx", "ty", None), P(), P())
    out_specs = (P("tx", "ty", None), P("tx", "ty", None, None, None))
    return jax.shard_map(local, mesh=mesh, in_specs=in_specs, out_specs=out_specs, check_vma=False)
```
